32 devices in a mesh: head: 4 (over y, x), seq: 8 (over z, core).
Axes of the slice: x: 2, y: 2, z: 4, core: 2. Of those that a mesh axis runs over, the one named last changes fastest.
Arguments:
- queries: bfloat16 [4096, 8192], P('seq', 'head'), may hold values from -200 to 200
- keys: bfloat16 [4096, 8192], P('seq', 'head'), may hold values from -6 to 6
- values: bfloat16 [4096, 8192], P('seq', 'head'), may hold values from -6 to 6
- cotangent: bfloat16 [4096, 8192], P('seq', 'head'), may hold values from -6 to 6
- prefix_keys: bfloat16 [4096, 8192], P('seq', 'head'), may hold values from -1.5 to 1.5
- prefix_values: bfloat16 [4096, 8192], P('seq', 'head'), may hold values from -1.5 to 1.5
- gain: float32 [8192], P('head'), may hold values from 0.5 to 1.5
- lengths: int32 [8], P('seq'), may hold values from 64 to 512, as said below
Outputs:
- normed: bfloat16 [4096, 8192], P('seq', 'head')
- query_grad: bfloat16 [4096, 8192], P('seq', 'head')
- key_grad: bfloat16 [4096, 8192], P('seq', 'head')
- value_grad: bfloat16 [4096, 8192], P('seq', 'head')
- prefix_key_grad: bfloat16 [4096, 8192], P('seq', 'head')
- prefix_value_grad: bfloat16 [4096, 8192], P('seq', 'head')
The draws below stay inside these ranges and needn't reach their ends.
Inputs may be any that keep to these rules, and one draw needn't show every extreme that they name: `lengths`: one length per response; some response has exactly 512 live slots and some exactly 64.
All inputs are finite; a program needn't handle non-finite values.
Results may differ from the reference program's by a relative error of at most 0.0058.
Values sent between devices are 32-bit elements; how exact they have to be, the bound alone decides.
A program may use at most 128 MiB of HBM per device.

```python
import jax
import jax.numpy as jnp
from jax import lax

H = 64
HEAD_DIM = 128
BLOCK = 256
RMAX = 512
RESP = 8
PRE = 4096
RTOK = 4096
WIDTH = 8192


def draw_queries(key, part):
    key_head, key_row, key_base = jax.random.split(key, 3)
    col_head = lax.iota(jnp.int32, WIDTH) // HEAD_DIM
    head_factor = jax.random.uniform(key_head, (H,), jnp.float32, 0.8, 1.2)
    head_scale = 10.0 ** (col_head.astype(jnp.float32) / max(H - 1, 1)) * head_factor[col_head]
    row_scale = 10.0 ** jax.random.uniform(key_row, (RTOK, 1), jnp.float32)
    base = jax.random.normal(key_base, (RTOK, WIDTH), jnp.float32)
    return jnp.clip(base * head_scale[None, :] * row_scale, -200.0, 200.0).astype(jnp.bfloat16)


def draw_lengths(key, part):
    key_len, key_shuffle = jax.random.split(key)
    drawn = jax.random.randint(key_len, (RESP,), RMAX // 8, RMAX + 1)
    shuffled = jax.random.permutation(key_shuffle, RESP)
    return drawn.at[shuffled[0]].set(RMAX).at[shuffled[1]].set(RMAX // 8)


def block_scale(key, extent, cuts, low, high):
    loudness = 1.0
    for position, blocks in cuts:
        steps = jax.random.uniform(jax.random.fold_in(jax.random.fold_in(key, 6), position), (blocks,), jnp.float32, low / len(cuts), high / len(cuts))
        loudness = loudness * jnp.repeat(jnp.exp(steps), extent[position] // blocks).reshape((-1,) + (1,) * (len(extent) - 1 - position))
    return loudness


def gaussian(stream_key, dims, scale, reach, shards=(), dtype=jnp.bfloat16):
    level = block_scale(stream_key, dims, shards, -0.22, 0.18) if shards else 1.0
    result = jax.random.normal(stream_key, dims, jnp.float32) * scale * level
    return jnp.minimum(jnp.maximum(result, -reach), reach).astype(dtype)


def setup_inputs(seed: int = 0) -> dict:
    streams_of = jax.random.split(jax.random.key(seed), 9)
    return {
        "queries": draw_queries(jax.random.fold_in(streams_of[8], 71), 0),
        "keys": gaussian(streams_of[1], (RTOK, WIDTH), 1.0, 6.0, ((0, 8), (1, 4))),
        "values": gaussian(streams_of[2], (RTOK, WIDTH), 1.0, 6.0, ((0, 8), (1, 4))),
        "cotangent": gaussian(streams_of[3], (RTOK, WIDTH), 1.0, 6.0, ((0, 8), (1, 4))),
        "prefix_keys": gaussian(streams_of[4], (PRE, WIDTH), 0.25, 1.5, ((0, 8), (1, 4))),
        "prefix_values": gaussian(streams_of[5], (PRE, WIDTH), 0.25, 1.5, ((0, 8), (1, 4))),
        "gain": jnp.clip(1.0 + 0.1 * jax.random.normal(streams_of[6], (WIDTH,), jnp.float32), 0.5, 1.5),
        "lengths": draw_lengths(jax.random.fold_in(streams_of[8], 71), 0),
    }


epsilon = 1e-06

def rounded(value):
    return lax.optimization_barrier(value.astype(jnp.bfloat16)).astype(jnp.float32)

def reference(queries, keys, values, cotangent, prefix_keys, prefix_values, gain, lengths):
    pre_keys = prefix_keys.astype(jnp.float32).reshape(PRE, H, HEAD_DIM)
    pre_values = prefix_values.astype(jnp.float32).reshape(PRE, H, HEAD_DIM)
    prefix_state = jnp.einsum('thd,the->hde', pre_keys, pre_values)
    causal = jnp.tril(jnp.ones((BLOCK, BLOCK), jnp.float32))
    block_count = RMAX // BLOCK

    def respond(pieces):
        q_in, k_in, v_in, cot_in, length = pieces
        live_mask = (jnp.arange(RMAX) < length).astype(jnp.bfloat16)[:, None]

        def shaped(array):
            return (array * live_mask).astype(jnp.float32).reshape(block_count, BLOCK, H, HEAD_DIM)
        q_live = shaped(q_in)
        k_live = shaped(k_in)
        v_live = shaped(v_in)

        def forward(state_now, blocks):
            q_block, k_block, v_block = blocks
            state_bf = rounded(state_now)
            from_state = jnp.einsum('bhd,hde->bhe', q_block, state_bf)
            scores = rounded(jnp.einsum('bhd,shd->hbs', q_block, k_block) * causal)
            in_block = jnp.einsum('hbs,she->bhe', scores, v_block)
            state_next = state_now + jnp.einsum('bhd,bhe->hde', k_block, v_block)
            return (state_next, (from_state + in_block, scores, state_bf))
        final_state, (attended, scores_all, states_all) = lax.scan(forward, prefix_state, (q_live, k_live, v_live))
        attended = attended.reshape(RMAX, WIDTH)
        root_mean = jnp.sqrt(lax.optimization_barrier(jnp.sum(attended * attended, axis=1)) / WIDTH + epsilon)[:, None]
        normed = (gain * attended / root_mean).astype(jnp.bfloat16)
        scaled_cot = gain * (cot_in * live_mask).astype(jnp.float32)
        inner_sum = lax.optimization_barrier(jnp.sum(scaled_cot * attended, axis=1))[:, None]
        out_grad = rounded(scaled_cot / root_mean - attended * inner_sum / (WIDTH * root_mean ** 3))
        out_grad = out_grad.reshape(block_count, BLOCK, H, HEAD_DIM)

        def backward(grad_state, blocks):
            q_block, k_block, v_block, d_block, scores, state_bf = blocks
            grad_bf = rounded(grad_state)
            pscore = rounded(jnp.einsum('bhe,she->hbs', d_block, v_block) * causal)
            grad_q = jnp.einsum('bhe,hde->bhd', d_block, state_bf) + jnp.einsum('hbs,shd->bhd', pscore, k_block)
            grad_k = jnp.einsum('bhe,hde->bhd', v_block, grad_bf) + jnp.einsum('hbs,bhd->shd', pscore, q_block)
            grad_v = jnp.einsum('bhd,hde->bhe', k_block, grad_bf) + jnp.einsum('hbs,bhe->she', scores, d_block)
            grad_next = grad_state + jnp.einsum('bhd,bhe->hde', q_block, d_block)
            return (grad_next, (grad_q, grad_k, grad_v))
        grad_zero = jnp.zeros((H, HEAD_DIM, HEAD_DIM), jnp.float32)
        grad_total, (grad_q, grad_k, grad_v) = lax.scan(backward, grad_zero, (q_live, k_live, v_live, out_grad, scores_all, states_all), reverse=True)
        flat = (normed, grad_q.reshape(RMAX, WIDTH).astype(jnp.bfloat16), grad_k.reshape(RMAX, WIDTH).astype(jnp.bfloat16), grad_v.reshape(RMAX, WIDTH).astype(jnp.bfloat16))
        return (flat, grad_total)
    (normed, query_grad, key_grad, value_grad), state_grads = lax.map(respond, (queries.reshape(RESP, RMAX, WIDTH), keys.reshape(RESP, RMAX, WIDTH), values.reshape(RESP, RMAX, WIDTH), cotangent.reshape(RESP, RMAX, WIDTH), lengths))
    state_grad = lax.optimization_barrier(jnp.sum(state_grads, axis=0))
    prefix_key_grad = jnp.einsum('the,hde->thd', pre_values, state_grad, precision=lax.Precision.HIGHEST).reshape(PRE, WIDTH).astype(jnp.bfloat16)
    prefix_value_grad = jnp.einsum('thd,hde->the', pre_keys, state_grad, precision=lax.Precision.HIGHEST).reshape(PRE, WIDTH).astype(jnp.bfloat16)
    return (normed.reshape(RTOK, WIDTH), query_grad.reshape(RTOK, WIDTH), key_grad.reshape(RTOK, WIDTH), value_grad.reshape(RTOK, WIDTH), prefix_key_grad, prefix_value_grad)
```

```python
import functools

import jax
import jax.numpy as jnp
from jax import lax
from jax.experimental import pallas as pl
from jax.experimental.pallas import tpu as pltpu
from jax.sharding import PartitionSpec as P

HEAD_DIM = 128
BLOCK = 256
EPS = 1e-06
MESH = pl.DeviceIdType.MESH
F32 = jnp.float32
BF16 = jnp.bfloat16
LEAD = 2
SKEW = 2


def mm(a, b, ca, cb):
    return lax.dot_general(a, b, (((ca,), (cb,)), ((), ())), preferred_element_type=F32)


def kernel(nh, ns, width, *refs):
    (q_hbm, k_hbm, v_hbm, dy_hbm, pk_hbm, pv_hbm, gain_ref, len_ref) = refs[:8]
    outs = refs[8:14]
    (q, k, v, dy, pk, pv, do, o, sc, mask, kv, mb, gb, sq, inn, rinv, coef) = refs[14:31]
    stage = refs[31:37]
    st_out, st_in = refs[37:39]
    bufs = (refs[39:46], refs[46:53])
    in_sem, out_sem, st_send, st_recv, send_sem, recv_sem = refs[53:59]

    rows, cols = q.shape
    heads = cols // HEAD_DIM
    nown = heads // 2
    nb = rows // BLOCK
    nz = ns // 2
    me_h = lax.axis_index("head")
    me_s = lax.axis_index("seq")
    z = me_s // 2
    core = me_s % 2
    own0 = core * nown
    oth0 = (1 - core) * nown
    partner = (me_h, z * 2 + 1 - core)
    right = (me_h, jnp.minimum(me_s + 2, ns - 1))
    left = (me_h, jnp.maximum(me_s - 2, 0))
    not_first = z > 0
    not_last = z < nz - 1

    def cs(h):
        return pl.ds(pl.multiple_of(h * HEAD_DIM, HEAD_DIM), HEAD_DIM)

    half = nown * HEAD_DIM

    def load_half(j, src, dst, first):
        c = pl.ds(pl.multiple_of(first * HEAD_DIM, HEAD_DIM), half)
        return pltpu.make_async_copy(src.at[:, c], dst.at[:, c], in_sem.at[j])

    loads = [
        load_half(0, pk_hbm, pk, oth0),
        load_half(1, pv_hbm, pv, oth0),
        load_half(2, pk_hbm, pk, own0),
        load_half(3, pv_hbm, pv, own0),
        pltpu.make_async_copy(q_hbm, q, in_sem.at[4]),
        pltpu.make_async_copy(k_hbm, k, in_sem.at[5]),
        pltpu.make_async_copy(v_hbm, v, in_sem.at[6]),
        pltpu.make_async_copy(dy_hbm, dy, in_sem.at[7]),
    ]
    for c in loads:
        c.start()

    barrier = pltpu.get_barrier_semaphore()
    pl.semaphore_signal(barrier, inc=1, device_id=partner, device_id_type=MESH)

    @pl.when(not_first)
    def _():
        pl.semaphore_signal(barrier, inc=1, device_id=left, device_id_type=MESH)

    @pl.when(not_last)
    def _():
        pl.semaphore_signal(barrier, inc=1, device_id=right, device_id_type=MESH)

    for d in range(1, nh):
        pl.semaphore_signal(
            barrier, inc=1, device_id=((me_h + d) % nh, me_s), device_id_type=MESH
        )

    live = lax.broadcasted_iota(jnp.int32, (rows, HEAD_DIM), 0) < len_ref[0]
    mask[...] = jnp.where(live, 1.0, 0.0).astype(BF16)
    sq[...] = jnp.zeros_like(sq)
    inn[...] = jnp.zeros_like(inn)
    pl.semaphore_wait(
        barrier, nh + not_first.astype(jnp.int32) + not_last.astype(jnp.int32)
    )
    for c in loads[:4]:
        c.wait()

    def causal():
        r = lax.broadcasted_iota(jnp.int32, (BLOCK, BLOCK), 0)
        c = lax.broadcasted_iota(jnp.int32, (BLOCK, BLOCK), 1)
        return r >= c

    def exchange(ph, produce, compute, consume):
        xo, xi, x, rin, rout, lin, lout_t = bufs[ph][:7]
        lout = lout_t.at[0]
        tot = lout_t.at[1]
        tin = lout_t.at[2]

        def hop(kind, src, dst, i, dev):
            return pltpu.make_async_remote_copy(
                src_ref=src.at[i],
                dst_ref=dst.at[i],
                send_sem=send_sem.at[ph, kind, i],
                recv_sem=recv_sem.at[ph, kind, i],
                device_id=dev,
                device_id_type=MESH,
            )

        def to_partner(i):
            return hop(0, xo, xi, i, partner)

        def to_right(i):
            return hop(1, rout, rin, i, right)

        def to_left(i):
            return hop(2, lout, lin, i, left)

        def total_out(i):
            return hop(3, tot, tin, i, partner)

        def give(i):
            xo[i] = produce(oth0 + i)
            to_partner(i).start()

        def first(i, carry):
            give(i)
            return carry

        lax.fori_loop(0, LEAD, first, 0)
        far = jnp.maximum(z, nz - 1 - z)
        late = max(SKEW * (nz - 1) + SKEW, nown)
        slots = max(heads, nown + late)

        def slot(s, carry):
            @pl.when(s + LEAD < nown)
            def _():
                give(s + LEAD)

            @pl.when(s < nown)
            def _():
                mine = produce(own0 + s)
                to_partner(s).wait_recv()
                x[s] = mine + xi[s]

            i_r = s - SKEW * z

            @pl.when((i_r >= 0) & (i_r < nown))
            def _():
                @pl.when(not_first)
                def _():
                    to_right(i_r).wait_recv()
                    rout[i_r] = rin[i_r] + x[i_r]

                @pl.when(jnp.logical_not(not_first))
                def _():
                    rout[i_r] = x[i_r]

                @pl.when(not_last)
                def _():
                    to_right(i_r).start()

            i_l = s - SKEW * (nz - 1 - z)

            @pl.when((i_l >= 0) & (i_l < nown))
            def _():
                @pl.when(not_last)
                def _():
                    to_left(i_l).wait_recv()
                    lout[i_l] = lin[i_l] + x[i_l]

                @pl.when(jnp.logical_not(not_last))
                def _():
                    lout[i_l] = x[i_l]

                @pl.when(not_first)
                def _():
                    to_left(i_l).start()

            i_t = s - SKEW * far

            @pl.when((i_t >= 0) & (i_t < nown))
            def _():
                @pl.when(not_last)
                def _():
                    tot[i_t] = rout[i_t] + lin[i_t]

                @pl.when(jnp.logical_not(not_last))
                def _():
                    tot[i_t] = rout[i_t]

                total_out(i_t).start()

            @pl.when(s < heads)
            def _():
                compute((own0 + s) % heads)

            @pl.when((i_t >= 0) & (i_t < nown))
            def _():
                consume(own0 + i_t, tot[i_t])

            i_o = s - late

            @pl.when((i_o >= 0) & (i_o < nown))
            def _():
                total_out(i_o).wait_recv()
                consume(oth0 + i_o, tin[i_o])

            return carry

        lax.fori_loop(0, slots, slot, 0)

        def drain(i, carry):
            to_partner(i).wait_send()
            total_out(i).wait_send()

            @pl.when(not_last)
            def _():
                to_right(i).wait_send()

            @pl.when(not_first)
            def _():
                to_left(i).wait_send()

            return carry

        lax.fori_loop(0, nown, drain, 0)

    def blk(ref, c, h):
        return ref[pl.ds(c * BLOCK, BLOCK), cs(h)]

    def prefix_part(h):
        return mm(pk[:, cs(h)], pv[:, cs(h)], 0, 0)

    def intra(h):
        m = mask[...]
        q[:, cs(h)] = q[:, cs(h)] * m
        k[:, cs(h)] = k[:, cs(h)] * m
        v[:, cs(h)] = v[:, cs(h)] * m
        run = None
        for c in range(nb):
            kc, vc = blk(k, c, h), blk(v, c, h)
            a = jnp.where(causal(), mm(blk(q, c, h), kc, 1, 1), 0.0).astype(BF16)
            sc[h, c] = a
            o[pl.ds(c * BLOCK, BLOCK), cs(h)] = mm(a, vc, 1, 0)
            if c < nb - 1:
                add = mm(kc, vc, 0, 0)
                run = add if run is None else run + add
                kv[h, c] = run

    def first_intra(h):
        intra(h)

    def use_state(h, state):
        g = gain_ref[:, cs(h)]
        for c in range(nb):
            st = (state if c == 0 else state + kv[h, c - 1]).astype(BF16)
            mb[h, c] = st
            r = pl.ds(c * BLOCK, BLOCK)
            oc = o[r, cs(h)] + mm(blk(q, c, h), st, 1, 0)
            o[r, cs(h)] = oc
            dm = blk(dy, c, h) * mask[r, :]
            dy[r, cs(h)] = dm
            sq[r, :] += oc * oc
            inn[r, :] += dm.astype(F32) * g * oc

    for c in loads[4:]:
        c.wait()
    exchange(0, prefix_part, first_intra, use_state)

    row_sq = jnp.sum(sq[...].T, axis=0, keepdims=True)
    row_in = jnp.sum(inn[...].T, axis=0, keepdims=True)
    st_out[...] = jnp.concatenate(
        [jnp.broadcast_to(row_sq, (4, rows)), jnp.broadcast_to(row_in, (4, rows))], axis=0
    )
    copies = []
    for d in range(1, nh):
        copies.append(
            pltpu.make_async_remote_copy(
                src_ref=st_out,
                dst_ref=st_in.at[d - 1],
                send_sem=st_send.at[d - 1],
                recv_sem=st_recv.at[d - 1],
                device_id=((me_h + d) % nh, me_s),
                device_id_type=MESH,
            )
        )
        copies[-1].start()
    total = st_out[...]
    for d in range(1, nh):
        copies[d - 1].wait_recv()
        total = total + st_in[d - 1]
    inv = 1.0 / jnp.sqrt(total[0:1] / width + EPS)
    cf = total[4:5] * (inv * inv * inv) / width
    rinv[...] = jnp.broadcast_to(inv, (HEAD_DIM, rows)).T
    coef[...] = jnp.broadcast_to(cf, (HEAD_DIM, rows)).T

    def put(j, h):
        pltpu.make_async_copy(
            stage[j].at[:, cs(h)], outs[j].at[:, cs(h)], out_sem.at[j]
        ).start()

    def state_grad(h):
        g = gain_ref[:, cs(h)]
        run = None
        for c in reversed(range(nb)):
            r = pl.ds(c * BLOCK, BLOCK)
            oc = o[r, cs(h)]
            ri = rinv[r, :]
            stage[0][r, cs(h)] = (g * oc * ri).astype(BF16)
            d = (blk(dy, c, h).astype(F32) * g * ri - oc * coef[r, :]).astype(BF16)
            do[r, cs(h)] = d
            if c < nb - 1:
                gb[h, c] = run.astype(BF16)
            part = mm(blk(q, c, h), d, 0, 0)
            run = part if run is None else run + part
        put(0, h)
        return run

    def grads(h):
        for c in range(nb):
            r = pl.ds(c * BLOCK, BLOCK)
            qc, kc, vc, dc = blk(q, c, h), blk(k, c, h), blk(v, c, h), blk(do, c, h)
            a = sc[h, c]
            p = jnp.where(causal(), mm(dc, vc, 1, 1), 0.0).astype(BF16)
            stage[1][r, cs(h)] = (mm(dc, mb[h, c], 1, 1) + mm(p, kc, 1, 0)).astype(BF16)
            kg = mm(p, qc, 0, 0)
            vg = mm(a, dc, 0, 0)
            if c < nb - 1:
                g = gb[h, c]
                kg = kg + mm(vc, g, 1, 1)
                vg = vg + mm(kc, g, 1, 0)
            stage[2][r, cs(h)] = kg.astype(BF16)
            stage[3][r, cs(h)] = vg.astype(BF16)
        put(1, h)
        put(2, h)
        put(3, h)

    def prefix_grads(h, state):
        hi = state.astype(BF16)
        lo = (state - hi.astype(F32)).astype(BF16)
        vals = pv[:, cs(h)]
        keys = pk[:, cs(h)]
        vv = jnp.concatenate([vals, vals], axis=1)
        kk = jnp.concatenate([keys, keys], axis=1)
        stage[4][:, cs(h)] = mm(vv, jnp.concatenate([hi, lo], axis=1), 1, 1).astype(BF16)
        stage[5][:, cs(h)] = mm(kk, jnp.concatenate([hi, lo], axis=0), 1, 0).astype(BF16)
        put(4, h)
        put(5, h)

    exchange(1, state_grad, grads, prefix_grads)
    for c in copies:
        c.wait_send()
    for j in range(6):
        pltpu.make_async_copy(stage[j], outs[j], out_sem.at[j]).wait()


def body(nh, ns, queries, keys, values, cotangent, prefix_keys, prefix_values, gain, lengths):
    rows, cols = queries.shape
    heads = cols // HEAD_DIM
    nown = heads // 2
    nb = rows // BLOCK
    any_spec = pl.BlockSpec(memory_space=pl.ANY)
    big = pltpu.VMEM((rows, cols), BF16)
    row = pltpu.VMEM((rows, HEAD_DIM), F32)
    st = pltpu.VMEM((nown, HEAD_DIM, HEAD_DIM), F32)
    states = [st, st, st, st, st, st, pltpu.VMEM((3, nown, HEAD_DIM, HEAD_DIM), F32)]
    scratch = (
        [big] * 7
        + [
            pltpu.VMEM((rows, cols), F32),
            pltpu.VMEM((heads, nb, BLOCK, BLOCK), BF16),
            pltpu.VMEM((rows, HEAD_DIM), BF16),
            pltpu.VMEM((heads, max(nb - 1, 1), HEAD_DIM, HEAD_DIM), F32),
            pltpu.VMEM((heads, nb, HEAD_DIM, HEAD_DIM), BF16),
            pltpu.VMEM((heads, max(nb - 1, 1), HEAD_DIM, HEAD_DIM), BF16),
            row,
            row,
            row,
            row,
        ]
        + [big] * 6
        + [pltpu.VMEM((8, rows), F32), pltpu.VMEM((max(nh - 1, 1), 8, rows), F32)]
        + states
        + states
        + [
            pltpu.SemaphoreType.DMA((8,)),
            pltpu.SemaphoreType.DMA((6,)),
            pltpu.SemaphoreType.DMA((max(nh - 1, 1),)),
            pltpu.SemaphoreType.DMA((max(nh - 1, 1),)),
            pltpu.SemaphoreType.DMA((2, 4, nown)),
            pltpu.SemaphoreType.DMA((2, 4, nown)),
        ]
    )
    out = jax.ShapeDtypeStruct((rows, cols), BF16)
    return tuple(
        pl.pallas_call(
            functools.partial(kernel, nh, ns, float(cols * nh)),
            out_shape=[out] * 6,
            in_specs=[any_spec] * 6
            + [
                pl.BlockSpec(memory_space=pltpu.VMEM),
                pl.BlockSpec(memory_space=pltpu.SMEM),
            ],
            out_specs=[any_spec] * 6,
            scratch_shapes=scratch,
            compiler_params=pltpu.CompilerParams(
                collective_id=0, has_side_effects=True, vmem_limit_bytes=60 * 1024 * 1024
            ),
        )(
            queries,
            keys,
            values,
            cotangent,
            prefix_keys,
            prefix_values,
            gain.reshape(1, cols),
            lengths,
        )
    )


def solution(mesh):
    nh, ns = mesh.shape["head"], mesh.shape["seq"]
    tok = P("seq", "head")
    return jax.shard_map(
        functools.partial(body, nh, ns),
        mesh=mesh,
        in_specs=(tok,) * 6 + (P("head"), P("seq")),
        out_specs=(tok,) * 6,
        check_vma=False,
    )
```

```python
import functools

import jax
import jax.numpy as jnp
from jax import lax
from jax.experimental import pallas as pl
from jax.experimental.pallas import tpu as pltpu
from jax.sharding import PartitionSpec as P

HEAD_DIM = 128
BLOCK = 256
EPS = 1e-06
MESH = pl.DeviceIdType.MESH
F32 = jnp.float32
BF16 = jnp.bfloat16
LEAD = 2
SKEW = 2


def mm(a, b, ca, cb):
    return lax.dot_general(a, b, (((ca,), (cb,)), ((), ())), preferred_element_type=F32)


def kernel(nh, ns, width, *refs):
    (q_hbm, k_hbm, v_hbm, dy_hbm, pk_hbm, pv_hbm, gain_ref, len_ref) = refs[:8]
    stage = refs[8:12]
    pk, pv, tout = refs[12:15]
    (q, k, v, dy, do, o, sc, mask, kv, mb, gb, sq, inn, rinv, coef) = refs[15:30]
    st_out, st_in = refs[30:32]
    bufs = (refs[32:39], refs[39:46])
    in_sem, st_send, st_recv, send_sem, recv_sem = refs[46:51]

    rows, cols = q.shape
    heads = cols // HEAD_DIM
    nown = heads // 2
    nb = rows // BLOCK
    nz = ns // 2
    me_h = lax.axis_index("head")
    me_s = lax.axis_index("seq")
    z = me_s // 2
    core = me_s % 2
    own0 = core * nown
    oth0 = (1 - core) * nown
    partner = (me_h, z * 2 + 1 - core)
    right = (me_h, jnp.minimum(me_s + 2, ns - 1))
    left = (me_h, jnp.maximum(me_s - 2, 0))
    not_first = z > 0
    not_last = z < nz - 1

    def cs(h):
        return pl.ds(pl.multiple_of(h * HEAD_DIM, HEAD_DIM), HEAD_DIM)

    half = nown * HEAD_DIM

    def load_half(j, src, dst, first):
        c = pl.ds(pl.multiple_of(first * HEAD_DIM, HEAD_DIM), half)
        return pltpu.make_async_copy(src.at[:, c], dst.at[:, c], in_sem.at[j])

    loads = [
        load_half(0, pk_hbm, pk, oth0),
        load_half(1, pv_hbm, pv, oth0),
        load_half(2, pk_hbm, pk, own0),
        load_half(3, pv_hbm, pv, own0),
        pltpu.make_async_copy(q_hbm, q, in_sem.at[4]),
        pltpu.make_async_copy(k_hbm, k, in_sem.at[5]),
        pltpu.make_async_copy(v_hbm, v, in_sem.at[6]),
        pltpu.make_async_copy(dy_hbm, dy, in_sem.at[7]),
    ]
    for c in loads:
        c.start()

    barrier = pltpu.get_barrier_semaphore()
    pl.semaphore_signal(barrier, inc=1, device_id=partner, device_id_type=MESH)

    @pl.when(not_first)
    def _():
        pl.semaphore_signal(barrier, inc=1, device_id=left, device_id_type=MESH)

    @pl.when(not_last)
    def _():
        pl.semaphore_signal(barrier, inc=1, device_id=right, device_id_type=MESH)

    for d in range(1, nh):
        pl.semaphore_signal(
            barrier, inc=1, device_id=((me_h + d) % nh, me_s), device_id_type=MESH
        )

    live = lax.broadcasted_iota(jnp.int32, (rows, HEAD_DIM), 0) < len_ref[0]
    mask[...] = jnp.where(live, 1.0, 0.0).astype(BF16)
    sq[...] = jnp.zeros_like(sq)
    inn[...] = jnp.zeros_like(inn)
    pl.semaphore_wait(
        barrier, nh + not_first.astype(jnp.int32) + not_last.astype(jnp.int32)
    )
    for c in loads[:4]:
        c.wait()

    def causal():
        r = lax.broadcasted_iota(jnp.int32, (BLOCK, BLOCK), 0)
        c = lax.broadcasted_iota(jnp.int32, (BLOCK, BLOCK), 1)
        return r >= c

    def exchange(ph, produce, compute, consume):
        xo, xi, x, rin, rout, lin, lout_t = bufs[ph][:7]
        lout = lout_t.at[0]
        tot = lout_t.at[1]
        tin = lout_t.at[2]

        def hop(kind, src, dst, i, dev):
            return pltpu.make_async_remote_copy(
                src_ref=src.at[i],
                dst_ref=dst.at[i],
                send_sem=send_sem.at[ph, kind, i],
                recv_sem=recv_sem.at[ph, kind, i],
                device_id=dev,
                device_id_type=MESH,
            )

        def to_partner(i):
            return hop(0, xo, xi, i, partner)

        def to_right(i):
            return hop(1, rout, rin, i, right)

        def to_left(i):
            return hop(2, lout, lin, i, left)

        def total_out(i):
            return hop(3, tot, tin, i, partner)

        def give(i):
            xo[i] = produce(oth0 + i)
            to_partner(i).start()

        def first(i, carry):
            give(i)
            return carry

        lax.fori_loop(0, LEAD, first, 0)
        far = jnp.maximum(z, nz - 1 - z)
        late = max(SKEW * (nz - 1) + SKEW, nown)
        slots = max(heads, nown + late)

        def slot(s, carry):
            @pl.when(s + LEAD < nown)
            def _():
                give(s + LEAD)

            @pl.when(s < nown)
            def _():
                mine = produce(own0 + s)
                to_partner(s).wait_recv()
                x[s] = mine + xi[s]

            i_r = s - SKEW * z

            @pl.when((i_r >= 0) & (i_r < nown))
            def _():
                @pl.when(not_first)
                def _():
                    to_right(i_r).wait_recv()
                    rout[i_r] = rin[i_r] + x[i_r]

                @pl.when(jnp.logical_not(not_first))
                def _():
                    rout[i_r] = x[i_r]

                @pl.when(not_last)
                def _():
                    to_right(i_r).start()

            i_l = s - SKEW * (nz - 1 - z)

            @pl.when((i_l >= 0) & (i_l < nown))
            def _():
                @pl.when(not_last)
                def _():
                    to_left(i_l).wait_recv()
                    lout[i_l] = lin[i_l] + x[i_l]

                @pl.when(jnp.logical_not(not_last))
                def _():
                    lout[i_l] = x[i_l]

                @pl.when(not_first)
                def _():
                    to_left(i_l).start()

            i_t = s - SKEW * far

            @pl.when((i_t >= 0) & (i_t < nown))
            def _():
                @pl.when(not_last)
                def _():
                    tot[i_t] = rout[i_t] + lin[i_t]

                @pl.when(jnp.logical_not(not_last))
                def _():
                    tot[i_t] = rout[i_t]

                total_out(i_t).start()

            @pl.when(s < heads)
            def _():
                compute((own0 + s) % heads)

            @pl.when((i_t >= 0) & (i_t < nown))
            def _():
                consume(own0 + i_t, tot[i_t])

            i_o = s - late

            @pl.when((i_o >= 0) & (i_o < nown))
            def _():
                total_out(i_o).wait_recv()
                consume(oth0 + i_o, tin[i_o])

            return carry

        lax.fori_loop(0, slots, slot, 0)

        def drain(i, carry):
            to_partner(i).wait_send()
            total_out(i).wait_send()

            @pl.when(not_last)
            def _():
                to_right(i).wait_send()

            @pl.when(not_first)
            def _():
                to_left(i).wait_send()

            return carry

        lax.fori_loop(0, nown, drain, 0)

    def blk(ref, c, h):
        return ref[pl.ds(c * BLOCK, BLOCK), cs(h)]

    def prefix_part(h):
        return mm(pk[:, cs(h)], pv[:, cs(h)], 0, 0)

    def intra(h):
        m = mask[...]
        q[:, cs(h)] = q[:, cs(h)] * m
        k[:, cs(h)] = k[:, cs(h)] * m
        v[:, cs(h)] = v[:, cs(h)] * m
        run = None
        for c in range(nb):
            kc, vc = blk(k, c, h), blk(v, c, h)
            a = jnp.where(causal(), mm(blk(q, c, h), kc, 1, 1), 0.0).astype(BF16)
            sc[h, c] = a
            o[pl.ds(c * BLOCK, BLOCK), cs(h)] = mm(a, vc, 1, 0)
            if c < nb - 1:
                add = mm(kc, vc, 0, 0)
                run = add if run is None else run + add
                kv[h, c] = run

    def first_intra(h):
        intra(h)

    def use_state(h, state):
        g = gain_ref[:, cs(h)]
        for c in range(nb):
            st = (state if c == 0 else state + kv[h, c - 1]).astype(BF16)
            mb[h, c] = st
            r = pl.ds(c * BLOCK, BLOCK)
            oc = o[r, cs(h)] + mm(blk(q, c, h), st, 1, 0)
            o[r, cs(h)] = oc
            dm = blk(dy, c, h) * mask[r, :]
            dy[r, cs(h)] = dm
            sq[r, :] += oc * oc
            inn[r, :] += dm.astype(F32) * g * oc

    for c in loads[4:]:
        c.wait()
    exchange(0, prefix_part, first_intra, use_state)

    row_sq = jnp.sum(sq[...].T, axis=0, keepdims=True)
    row_in = jnp.sum(inn[...].T, axis=0, keepdims=True)
    st_out[...] = jnp.concatenate(
        [jnp.broadcast_to(row_sq, (4, rows)), jnp.broadcast_to(row_in, (4, rows))], axis=0
    )
    copies = []
    for d in range(1, nh):
        copies.append(
            pltpu.make_async_remote_copy(
                src_ref=st_out,
                dst_ref=st_in.at[d - 1],
                send_sem=st_send.at[d - 1],
                recv_sem=st_recv.at[d - 1],
                device_id=((me_h + d) % nh, me_s),
                device_id_type=MESH,
            )
        )
        copies[-1].start()
    total = st_out[...]
    for d in range(1, nh):
        copies[d - 1].wait_recv()
        total = total + st_in[d - 1]
    inv = 1.0 / jnp.sqrt(total[0:1] / width + EPS)
    cf = total[4:5] * (inv * inv * inv) / width
    rinv[...] = jnp.broadcast_to(inv, (HEAD_DIM, rows)).T
    coef[...] = jnp.broadcast_to(cf, (HEAD_DIM, rows)).T

    def state_grad(h):
        g = gain_ref[:, cs(h)]
        run = None
        for c in reversed(range(nb)):
            r = pl.ds(c * BLOCK, BLOCK)
            oc = o[r, cs(h)]
            ri = rinv[r, :]
            stage[0][r, cs(h)] = (g * oc * ri).astype(BF16)
            d = (blk(dy, c, h).astype(F32) * g * ri - oc * coef[r, :]).astype(BF16)
            do[r, cs(h)] = d
            if c < nb - 1:
                gb[h, c] = run.astype(BF16)
            part = mm(blk(q, c, h), d, 0, 0)
            run = part if run is None else run + part
        return run

    def grads(h):
        for c in range(nb):
            r = pl.ds(c * BLOCK, BLOCK)
            qc, kc, vc, dc = blk(q, c, h), blk(k, c, h), blk(v, c, h), blk(do, c, h)
            a = sc[h, c]
            p = jnp.where(causal(), mm(dc, vc, 1, 1), 0.0).astype(BF16)
            stage[1][r, cs(h)] = (mm(dc, mb[h, c], 1, 1) + mm(p, kc, 1, 0)).astype(BF16)
            kg = mm(p, qc, 0, 0)
            vg = mm(a, dc, 0, 0)
            if c < nb - 1:
                g = gb[h, c]
                kg = kg + mm(vc, g, 1, 1)
                vg = vg + mm(kc, g, 1, 0)
            stage[2][r, cs(h)] = kg.astype(BF16)
            stage[3][r, cs(h)] = vg.astype(BF16)

    def keep_total(h, state):
        tout[h] = state

    exchange(1, state_grad, grads, keep_total)
    for c in copies:
        c.wait_send()


def finish(*refs):
    ready = refs[:4]
    pk, pv, total = refs[4:7]
    outs = refs[7:13]
    pkg, pvg, sem = refs[13:16]
    heads = total.shape[0]
    for j in range(4):
        pltpu.make_async_copy(ready[j], outs[j], sem.at[j]).start()

    def head(h, carry):
        c = pl.ds(pl.multiple_of(h * HEAD_DIM, HEAD_DIM), HEAD_DIM)
        state = total[h]
        hi = state.astype(BF16)
        lo = (state - hi.astype(F32)).astype(BF16)
        vals, keys = pv[:, c], pk[:, c]
        vv = jnp.concatenate([vals, vals], axis=1)
        kk = jnp.concatenate([keys, keys], axis=1)
        pkg[:, c] = mm(vv, jnp.concatenate([hi, lo], axis=1), 1, 1).astype(BF16)
        pvg[:, c] = mm(kk, jnp.concatenate([hi, lo], axis=0), 1, 0).astype(BF16)
        pltpu.make_async_copy(pkg.at[:, c], outs[4].at[:, c], sem.at[4]).start()
        pltpu.make_async_copy(pvg.at[:, c], outs[5].at[:, c], sem.at[5]).start()
        return carry

    lax.fori_loop(0, heads, head, 0)
    for j in range(4):
        pltpu.make_async_copy(ready[j], outs[j], sem.at[j]).wait()
    pltpu.make_async_copy(pkg, outs[4], sem.at[4]).wait()
    pltpu.make_async_copy(pvg, outs[5], sem.at[5]).wait()


def body(nh, ns, queries, keys, values, cotangent, prefix_keys, prefix_values, gain, lengths):
    rows, cols = queries.shape
    heads = cols // HEAD_DIM
    nown = heads // 2
    nb = rows // BLOCK
    any_spec = pl.BlockSpec(memory_space=pl.ANY)
    big = pltpu.VMEM((rows, cols), BF16)
    row = pltpu.VMEM((rows, HEAD_DIM), F32)
    st = pltpu.VMEM((nown, HEAD_DIM, HEAD_DIM), F32)
    states = [st, st, st, st, st, st, pltpu.VMEM((3, nown, HEAD_DIM, HEAD_DIM), F32)]
    scratch = (
        [big] * 5
        + [
            pltpu.VMEM((rows, cols), F32),
            pltpu.VMEM((heads, nb, BLOCK, BLOCK), BF16),
            pltpu.VMEM((rows, HEAD_DIM), BF16),
            pltpu.VMEM((heads, max(nb - 1, 1), HEAD_DIM, HEAD_DIM), F32),
            pltpu.VMEM((heads, nb, HEAD_DIM, HEAD_DIM), BF16),
            pltpu.VMEM((heads, max(nb - 1, 1), HEAD_DIM, HEAD_DIM), BF16),
            row,
            row,
            row,
            row,
        ]
        + [pltpu.VMEM((8, rows), F32), pltpu.VMEM((max(nh - 1, 1), 8, rows), F32)]
        + states
        + states
        + [
            pltpu.SemaphoreType.DMA((8,)),
            pltpu.SemaphoreType.DMA((max(nh - 1, 1),)),
            pltpu.SemaphoreType.DMA((max(nh - 1, 1),)),
            pltpu.SemaphoreType.DMA((2, 4, nown)),
            pltpu.SemaphoreType.DMA((2, 4, nown)),
        ]
    )
    fast = pl.BlockSpec(memory_space=pltpu.VMEM)
    tot = pltpu.VMEM((heads, HEAD_DIM, HEAD_DIM), F32)
    wide = [queries, keys, values, cotangent, prefix_keys, prefix_values]
    wide = [pltpu.with_memory_space_constraint(x, pltpu.HBM) for x in wide]
    made = pl.pallas_call(
        functools.partial(kernel, nh, ns, float(cols * nh)),
        out_shape=[big] * 6 + [tot],
        in_specs=[any_spec] * 6 + [fast, pl.BlockSpec(memory_space=pltpu.SMEM)],
        out_specs=[fast] * 7,
        scratch_shapes=scratch,
        compiler_params=pltpu.CompilerParams(
            collective_id=0, has_side_effects=True, vmem_limit_bytes=36 * 1024 * 1024
        ),
    )(*wide, gain.reshape(1, cols), lengths)
    made = [pltpu.with_memory_space_constraint(x, pltpu.VMEM) for x in made]
    out = pltpu.HBM((rows, cols), BF16)
    return tuple(
        pl.pallas_call(
            finish,
            out_shape=[out] * 6,
            in_specs=[fast] * 7,
            out_specs=[any_spec] * 6,
            scratch_shapes=[big, big, pltpu.SemaphoreType.DMA((6,))],
            compiler_params=pltpu.CompilerParams(vmem_limit_bytes=8 * 1024 * 1024),
        )(*made)
    )


def solution(mesh):
    nh, ns = mesh.shape["head"], mesh.shape["seq"]
    tok = P("seq", "head")
    return jax.shard_map(
        functools.partial(body, nh, ns),
        mesh=mesh,
        in_specs=(tok,) * 6 + (P("head"), P("seq")),
        out_specs=(tok,) * 6,
        check_vma=False,
    )
```

```python
import functools

import jax
import jax.numpy as jnp
from jax import lax
from jax.experimental import pallas as pl
from jax.experimental.pallas import tpu as pltpu
from jax.sharding import PartitionSpec as P

HEAD_DIM = 128
BLOCK = 256
EPS = 1e-06
MESH = pl.DeviceIdType.MESH
F32 = jnp.float32
BF16 = jnp.bfloat16
LEAD = 2
SUB = 1
SKEW = 3


def mm(a, b, ca, cb):
    return lax.dot_general(a, b, (((ca,), (cb,)), ((), ())), preferred_element_type=F32)


def kernel(nh, ns, width, *refs):
    (q_hbm, k_hbm, v_hbm, dy_hbm, pk_hbm, pv_hbm, gain_hbm, len_ref) = refs[:8]
    stage = refs[8:12]
    pk, pv, tout = refs[12:15]
    (q, k, v, dy, do, o, sc, mask, kv, mb, gb, sq, inn, rinv, coef) = refs[15:30]
    st_out, st_in = refs[30:32]
    bufs = (refs[32:41], refs[41:50])
    in_sem, st_send, st_recv, send_sem, recv_sem, gain_ref = refs[50:56]

    rows, cols = q.shape
    heads = cols // HEAD_DIM
    nown = heads // 2
    nb = rows // BLOCK
    nz = ns // 2
    me_h = lax.axis_index("head")
    me_s = lax.axis_index("seq")
    z = me_s // 2
    core = me_s % 2
    own0 = core * nown
    oth0 = (1 - core) * nown
    partner = (me_h, z * 2 + 1 - core)
    right = (me_h, jnp.minimum(me_s + 2, ns - 1))
    left = (me_h, jnp.maximum(me_s - 2, 0))
    not_first = z > 0
    not_last = z < nz - 1

    def cs(h):
        return pl.ds(pl.multiple_of(h * HEAD_DIM, HEAD_DIM), HEAD_DIM)

    half = nown * HEAD_DIM

    def load_half(j, src, dst, first):
        c = pl.ds(pl.multiple_of(first * HEAD_DIM, HEAD_DIM), half)
        return pltpu.make_async_copy(src.at[:, c], dst.at[:, c], in_sem.at[j])

    loads = [
        load_half(0, pk_hbm, pk, oth0),
        load_half(1, pv_hbm, pv, oth0),
        load_half(2, pk_hbm, pk, own0),
        load_half(3, pv_hbm, pv, own0),
        pltpu.make_async_copy(q_hbm, q, in_sem.at[4]),
        pltpu.make_async_copy(k_hbm, k, in_sem.at[5]),
        pltpu.make_async_copy(v_hbm, v, in_sem.at[6]),
        pltpu.make_async_copy(dy_hbm, dy, in_sem.at[7]),
        pltpu.make_async_copy(gain_hbm, gain_ref, in_sem.at[8]),
    ]
    for c in loads:
        c.start()

    barrier = pltpu.get_barrier_semaphore()
    pl.semaphore_signal(barrier, inc=1, device_id=partner, device_id_type=MESH)

    @pl.when(not_first)
    def _():
        pl.semaphore_signal(barrier, inc=1, device_id=left, device_id_type=MESH)

    @pl.when(not_last)
    def _():
        pl.semaphore_signal(barrier, inc=1, device_id=right, device_id_type=MESH)

    for d in range(1, nh):
        pl.semaphore_signal(
            barrier, inc=1, device_id=((me_h + d) % nh, me_s), device_id_type=MESH
        )

    live = lax.broadcasted_iota(jnp.int32, (rows, HEAD_DIM), 0) < len_ref[0]
    mask[...] = jnp.where(live, 1.0, 0.0).astype(BF16)
    sq[...] = jnp.zeros_like(sq)
    inn[...] = jnp.zeros_like(inn)
    pl.semaphore_wait(
        barrier, nh + not_first.astype(jnp.int32) + not_last.astype(jnp.int32)
    )
    for c in loads[:2]:
        c.wait()

    def causal():
        r = lax.broadcasted_iota(jnp.int32, (BLOCK, BLOCK), 0)
        c = lax.broadcasted_iota(jnp.int32, (BLOCK, BLOCK), 1)
        return r >= c

    def exchange(ph, produce, compute, consume, ready):
        xo, xi, x, rin, rout, lin, lout, tot, tin = bufs[ph]
        pieces = nown * SUB

        def hop(kind, src, dst, i, dev):
            return pltpu.make_async_remote_copy(
                src_ref=src,
                dst_ref=dst,
                send_sem=send_sem.at[ph, kind, i],
                recv_sem=recv_sem.at[ph, kind, i],
                device_id=dev,
                device_id_type=MESH,
            )

        def to_partner(i):
            return hop(0, xo.at[i], xi.at[i], i, partner)

        def total_out(i):
            return hop(1, tot.at[i], tin.at[i], i, partner)

        def to_right(i):
            return hop(2, rout.at[i // SUB, i % SUB], rin.at[i // SUB, i % SUB], i, right)

        def to_left(i):
            return hop(3, lout.at[i // SUB, i % SUB], lin.at[i // SUB, i % SUB], i, left)

        def split(state):
            return state.reshape(SUB, HEAD_DIM // SUB, HEAD_DIM)

        def give(i):
            xo[i] = split(produce(oth0 + i))
            to_partner(i).start()

        def first(i, carry):
            give(i)
            return carry

        lax.fori_loop(0, LEAD, first, 0)
        ready(-1)
        far = jnp.maximum(z, nz - 1 - z)
        late = max((SKEW * (nz - 1) + SUB - 1) // SUB + 2, nown)
        slots = max(heads, nown + late)

        def step(t):
            i_r = t - SKEW * z

            @pl.when((i_r >= 0) & (i_r < pieces))
            def _():
                i, j = i_r // SUB, i_r % SUB

                @pl.when(not_first)
                def _():
                    to_right(i_r).wait_recv()
                    rout[i, j] = rin[i, j] + x[i, j]

                @pl.when(jnp.logical_not(not_first))
                def _():
                    rout[i, j] = x[i, j]

                @pl.when(not_last)
                def _():
                    to_right(i_r).start()

            i_l = t - SKEW * (nz - 1 - z)

            @pl.when((i_l >= 0) & (i_l < pieces))
            def _():
                i, j = i_l // SUB, i_l % SUB

                @pl.when(not_last)
                def _():
                    to_left(i_l).wait_recv()
                    lout[i, j] = lin[i, j] + x[i, j]

                @pl.when(jnp.logical_not(not_last))
                def _():
                    lout[i, j] = x[i, j]

                @pl.when(not_first)
                def _():
                    to_left(i_l).start()

        def slot(s, carry):
            @pl.when(s + LEAD < nown)
            def _():
                give(s + LEAD)

            @pl.when(s < nown)
            def _():
                mine = split(produce(own0 + s))
                to_partner(s).wait_recv()
                x[s] = mine + xi[s]

            ready(s)
            for j in range(SUB):
                step(s * SUB + j)
                if j == 0:

                    @pl.when(s < heads)
                    def _():
                        for c in range(nb):
                            compute((own0 + s) % heads, c)

            i_t = s - (SKEW * far + SUB - 1) // SUB

            @pl.when((i_t >= 0) & (i_t < nown))
            def _():
                @pl.when(not_last)
                def _():
                    tot[i_t] = rout[i_t] + lin[i_t]

                @pl.when(jnp.logical_not(not_last))
                def _():
                    tot[i_t] = rout[i_t]

                total_out(i_t).start()
                consume(own0 + i_t, tot[i_t].reshape(HEAD_DIM, HEAD_DIM))

            i_o = s - late

            @pl.when((i_o >= 0) & (i_o < nown))
            def _():
                total_out(i_o).wait_recv()
                consume(oth0 + i_o, tin[i_o].reshape(HEAD_DIM, HEAD_DIM))

            return carry

        lax.fori_loop(0, slots, slot, 0)

        def drain(i, carry):
            to_partner(i).wait_send()
            total_out(i).wait_send()
            return carry

        lax.fori_loop(0, nown, drain, 0)

        def drain_hop(i, carry):
            @pl.when(not_last)
            def _():
                to_right(i).wait_send()

            @pl.when(not_first)
            def _():
                to_left(i).wait_send()

            return carry

        lax.fori_loop(0, pieces, drain_hop, 0)

    def blk(ref, c, h):
        return ref[pl.ds(c * BLOCK, BLOCK), cs(h)]

    def prefix_part(h):
        return mm(pk[:, cs(h)], pv[:, cs(h)], 0, 0)

    def intra(h, c):
        r = pl.ds(c * BLOCK, BLOCK)
        m = mask[r, :]
        qc, kc, vc = blk(q, c, h) * m, blk(k, c, h) * m, blk(v, c, h) * m
        q[r, cs(h)] = qc
        k[r, cs(h)] = kc
        v[r, cs(h)] = vc
        a = jnp.where(causal(), mm(qc, kc, 1, 1), 0.0).astype(BF16)
        sc[h, c] = a
        o[r, cs(h)] = mm(a, vc, 1, 0)
        if c < nb - 1:
            add = mm(kc, vc, 0, 0)
            kv[h, c] = add if c == 0 else kv[h, c - 1] + add

    def loaded(s):
        if isinstance(s, int):
            for c in loads[2:4]:
                c.wait()
            return

        @pl.when(s == 0)
        def _():
            for c in loads[4:7]:
                c.wait()

        @pl.when(s == 1)
        def _():
            loads[7].wait()
            loads[8].wait()

    def use_state(h, state):
        g = gain_ref[:, cs(h)]
        for c in range(nb):
            st = (state if c == 0 else state + kv[h, c - 1]).astype(BF16)
            mb[h, c] = st
            r = pl.ds(c * BLOCK, BLOCK)
            oc = o[r, cs(h)] + mm(blk(q, c, h), st, 1, 0)
            o[r, cs(h)] = oc
            dm = blk(dy, c, h) * mask[r, :]
            dy[r, cs(h)] = dm
            sq[r, :] += oc * oc
            inn[r, :] += dm.astype(F32) * g * oc

    exchange(0, prefix_part, intra, use_state, loaded)

    row_sq = jnp.sum(sq[...].T, axis=0, keepdims=True)
    row_in = jnp.sum(inn[...].T, axis=0, keepdims=True)
    st_out[...] = jnp.concatenate(
        [jnp.broadcast_to(row_sq, (4, rows)), jnp.broadcast_to(row_in, (4, rows))], axis=0
    )
    copies = []
    for d in range(1, nh):
        copies.append(
            pltpu.make_async_remote_copy(
                src_ref=st_out,
                dst_ref=st_in.at[d - 1],
                send_sem=st_send.at[d - 1],
                recv_sem=st_recv.at[d - 1],
                device_id=((me_h + d) % nh, me_s),
                device_id_type=MESH,
            )
        )
        copies[-1].start()
    total = st_out[...]
    for d in range(1, nh):
        copies[d - 1].wait_recv()
        total = total + st_in[d - 1]
    inv = 1.0 / jnp.sqrt(total[0:1] / width + EPS)
    cf = total[4:5] * (inv * inv * inv) / width
    rinv[...] = jnp.broadcast_to(inv, (HEAD_DIM, rows)).T
    coef[...] = jnp.broadcast_to(cf, (HEAD_DIM, rows)).T

    def state_grad(h):
        g = gain_ref[:, cs(h)]
        run = None
        for c in reversed(range(nb)):
            r = pl.ds(c * BLOCK, BLOCK)
            oc = o[r, cs(h)]
            ri = rinv[r, :]
            stage[0][r, cs(h)] = (g * oc * ri).astype(BF16)
            d = (blk(dy, c, h).astype(F32) * g * ri - oc * coef[r, :]).astype(BF16)
            do[r, cs(h)] = d
            if c < nb - 1:
                gb[h, c] = run.astype(BF16)
            part = mm(blk(q, c, h), d, 0, 0)
            run = part if run is None else run + part
        return run

    def grads(h, c):
        r = pl.ds(c * BLOCK, BLOCK)
        qc, kc, vc, dc = blk(q, c, h), blk(k, c, h), blk(v, c, h), blk(do, c, h)
        a = sc[h, c]
        p = jnp.where(causal(), mm(dc, vc, 1, 1), 0.0).astype(BF16)
        stage[1][r, cs(h)] = (mm(dc, mb[h, c], 1, 1) + mm(p, kc, 1, 0)).astype(BF16)
        kg = mm(p, qc, 0, 0)
        vg = mm(a, dc, 0, 0)
        if c < nb - 1:
            g = gb[h, c]
            kg = kg + mm(vc, g, 1, 1)
            vg = vg + mm(kc, g, 1, 0)
        stage[2][r, cs(h)] = kg.astype(BF16)
        stage[3][r, cs(h)] = vg.astype(BF16)

    def keep_total(h, state):
        tout[h] = state

    exchange(1, state_grad, grads, keep_total, lambda s: None)
    for c in copies:
        c.wait_send()


def finish(*refs):
    ready = refs[:4]
    pk, pv, total = refs[4:7]
    outs = refs[7:13]
    pkg, pvg, sem = refs[13:16]
    heads = total.shape[0]
    for j in range(4):
        pltpu.make_async_copy(ready[j], outs[j], sem.at[j]).start()

    def head(h, carry):
        c = pl.ds(pl.multiple_of(h * HEAD_DIM, HEAD_DIM), HEAD_DIM)
        state = total[h]
        hi = state.astype(BF16)
        lo = (state - hi.astype(F32)).astype(BF16)
        vals, keys = pv[:, c], pk[:, c]
        vv = jnp.concatenate([vals, vals], axis=1)
        kk = jnp.concatenate([keys, keys], axis=1)
        pkg[:, c] = mm(vv, jnp.concatenate([hi, lo], axis=1), 1, 1).astype(BF16)
        pvg[:, c] = mm(kk, jnp.concatenate([hi, lo], axis=0), 1, 0).astype(BF16)
        pltpu.make_async_copy(pkg.at[:, c], outs[4].at[:, c], sem.at[4]).start()
        pltpu.make_async_copy(pvg.at[:, c], outs[5].at[:, c], sem.at[5]).start()
        return carry

    lax.fori_loop(0, heads, head, 0)
    for j in range(4):
        pltpu.make_async_copy(ready[j], outs[j], sem.at[j]).wait()
    pltpu.make_async_copy(pkg, outs[4], sem.at[4]).wait()
    pltpu.make_async_copy(pvg, outs[5], sem.at[5]).wait()


def body(nh, ns, queries, keys, values, cotangent, prefix_keys, prefix_values, gain, lengths):
    rows, cols = queries.shape
    heads = cols // HEAD_DIM
    nown = heads // 2
    nb = rows // BLOCK
    any_spec = pl.BlockSpec(memory_space=pl.ANY)
    big = pltpu.VMEM((rows, cols), BF16)
    row = pltpu.VMEM((rows, HEAD_DIM), F32)
    states = [pltpu.VMEM((nown, SUB, HEAD_DIM // SUB, HEAD_DIM), F32)] * 9
    scratch = (
        [big] * 5
        + [
            pltpu.VMEM((rows, cols), F32),
            pltpu.VMEM((heads, nb, BLOCK, BLOCK), BF16),
            pltpu.VMEM((rows, HEAD_DIM), BF16),
            pltpu.VMEM((heads, max(nb - 1, 1), HEAD_DIM, HEAD_DIM), F32),
            pltpu.VMEM((heads, nb, HEAD_DIM, HEAD_DIM), BF16),
            pltpu.VMEM((heads, max(nb - 1, 1), HEAD_DIM, HEAD_DIM), BF16),
            row,
            row,
            row,
            row,
        ]
        + [pltpu.VMEM((8, rows), F32), pltpu.VMEM((max(nh - 1, 1), 8, rows), F32)]
        + states
        + states
        + [
            pltpu.SemaphoreType.DMA((9,)),
            pltpu.SemaphoreType.DMA((max(nh - 1, 1),)),
            pltpu.SemaphoreType.DMA((max(nh - 1, 1),)),
            pltpu.SemaphoreType.DMA((2, 4, nown * SUB)),
            pltpu.SemaphoreType.DMA((2, 4, nown * SUB)),
            pltpu.VMEM((1, cols), F32),
        ]
    )
    fast = pl.BlockSpec(memory_space=pltpu.VMEM)
    tot = pltpu.VMEM((heads, HEAD_DIM, HEAD_DIM), F32)
    wide = [queries, keys, values, cotangent, prefix_keys, prefix_values]
    wide.append(gain.reshape(1, cols))
    wide = [pltpu.with_memory_space_constraint(x, pltpu.HBM) for x in wide]
    made = pl.pallas_call(
        functools.partial(kernel, nh, ns, float(cols * nh)),
        out_shape=[big] * 6 + [tot],
        in_specs=[any_spec] * 7 + [pl.BlockSpec(memory_space=pltpu.SMEM)],
        out_specs=[fast] * 7,
        scratch_shapes=scratch,
        compiler_params=pltpu.CompilerParams(
            collective_id=0, has_side_effects=True, vmem_limit_bytes=36 * 1024 * 1024
        ),
    )(*wide, lengths)
    made = [pltpu.with_memory_space_constraint(x, pltpu.VMEM) for x in made]
    out = pltpu.HBM((rows, cols), BF16)
    return tuple(
        pl.pallas_call(
            finish,
            out_shape=[out] * 6,
            in_specs=[fast] * 7,
            out_specs=[any_spec] * 6,
            scratch_shapes=[big, big, pltpu.SemaphoreType.DMA((6,))],
            compiler_params=pltpu.CompilerParams(vmem_limit_bytes=8 * 1024 * 1024),
        )(*made)
    )


def solution(mesh):
    nh, ns = mesh.shape["head"], mesh.shape["seq"]
    tok = P("seq", "head")
    return jax.shard_map(
        functools.partial(body, nh, ns),
        mesh=mesh,
        in_specs=(tok,) * 6 + (P("head"), P("seq")),
        out_specs=(tok,) * 6,
        check_vma=False,
    )
```
